32 devices in a mesh: phase: 2 (over x), ctx: 8 (over z, core), mp: 2 (over y).
Axes of the slice: x: 2, y: 2, z: 4, core: 2. Of those that a mesh axis runs over, the one named last changes fastest.
Arguments:
- streams: bfloat16 [2, 1536, 3, 8192], P('phase', 'ctx', None, 'mp'), may hold values from -12 to 12
- doc_ids: int32 [1536], replicated, may hold values from 0 to 3, never falling along the last dimension, each value on 1 to 768 neighbouring positions
- feat_short: float32 [3, 3, 8192], P(None, None, 'mp'), may hold values from -3 to 3
- filt_short: float32 [7, 8192], P(None, 'mp'), may hold values from -2 to 2
- feat_medium: float32 [3, 3, 8192], P(None, None, 'mp'), may hold values from -3 to 3
- filt_medium: float32 [128, 8192], P(None, 'mp'), may hold values from -0.75 to 0.75
- medium_rates: float32 [8192], P('mp'), may hold values from 0.004 to 0.12
Outputs:
- next_state: bfloat16 [2, 1536, 3, 8192], P('phase', 'ctx', None, 'mp')
The draws below stay inside these ranges and needn't reach their ends.
Inputs may be any that keep to these rules, and one draw needn't show every extreme that they name: `doc_ids`: document ids never fall along the context, and no document is longer than half of 1536 positions.
All inputs are finite; a program needn't handle non-finite values.
Results may differ from the reference program's by a relative error of at most 0.008.
Values may be sent and summed in bfloat16 or wider, within the bound.
A program may use at most 192 MiB of HBM per device.

```python
import math
import jax
import jax.numpy as jnp
import numpy as np
from jax import lax

D = 8192
HEADS = 64
HEAD_DIM = 128
SE_LEN = 7
MR_LEN = 128
QBLOCK = 768
L = 1536


def draw_streams(key, part):
    shape = (2, L, 3, D)
    drawn = jnp.clip(jax.random.normal(key, shape, jnp.float32), -6.0, 6.0)
    return drawn.astype(jnp.bfloat16)


def steps_of(stream_key, extent, shards, smallest, largest):
    def one(axis_at, shards_of):
        heights = jax.random.uniform(jax.random.fold_in(jax.random.fold_in(stream_key, 6), axis_at), (shards_of,), jnp.float32, smallest / len(shards), largest / len(shards))
        return jnp.repeat(jnp.exp(heights), extent[axis_at] // shards_of).reshape((-1,) + (1,) * (len(extent) - axis_at - 1))

    level = one(*shards[0])
    for cut in shards[1:]:
        level = level * one(*cut)
    return level


def split_up(amount, total, bound, lean):
    weights = [(1 << 20) // math.isqrt(standing ** lean) + 1 for standing in range(2, amount + 1)]
    spare, counts = total - bound - (amount - 1), [1] * (amount - 1)
    while spare > 0:
        movable = [i for i in range(amount - 1) if counts[i] < bound]
        mass, left = sum([weights[i] for i in movable]), spare
        for i in movable:
            addition = min(bound - counts[i], max(1, left * weights[i] // mass), spare)
            counts[i] = counts[i] + addition
            spare = spare - addition
    return np.array([bound] + counts)


def ragged(key, amount, total, reach, lean):
    if amount == 2:
        one = jax.random.randint(key, (), max(1, total - reach), min(reach, total - 1) + 1)
        return jnp.stack([one, total - one])
    sizes = jnp.asarray(split_up(amount, total, reach, lean), jnp.int32)
    couples = (amount - 1) // 2
    giver, taker = sizes[1:1 + 2 * couples:2], sizes[2:2 + 2 * couples:2]
    margin = jnp.minimum(giver - 1, reach - taker)
    moved = jax.random.randint(jax.random.fold_in(key, 1), (couples,), 0, 1 << 20) % (margin + 1)
    sizes = sizes.at[1:1 + 2 * couples:2].set(giver - moved).at[2:2 + 2 * couples:2].set(taker + moved)
    return sizes[jax.random.permutation(jax.random.fold_in(key, 2), amount)]


def scatter_about(key, extent, spread, reach, cuts=(), kind=jnp.bfloat16):
    array = jax.random.normal(key, extent, jnp.float32) * spread
    if len(cuts) > 0:
        array = steps_of(key, extent, cuts, -0.22, 0.18) * array
    return jnp.clip(array, min=-reach, max=reach).astype(kind)


def setup_inputs(seed: int = 0) -> dict:
    keys = jax.random.split(jax.random.key(seed), 8)
    streams = draw_streams(jax.random.fold_in(keys[7], 71), 0)
    doc_ids = jnp.searchsorted(jnp.cumsum(ragged(keys[1], 4, L, L // 2, 0)), jnp.arange(L), side="right").astype(jnp.int32)
    feat_short = scatter_about(keys[2], (3, 3, D), 0.6, 3.0, ((2, 2),), jnp.float32)
    filt_short = scatter_about(keys[3], (SE_LEN, D), SE_LEN ** -0.5, 2.0, ((1, 2),), jnp.float32)
    feat_medium = scatter_about(keys[4], (3, 3, D), 0.6, 3.0, ((2, 2),), jnp.float32)
    filt_medium = scatter_about(keys[5], (MR_LEN, D), (MR_LEN // 2) ** -0.5, 0.75, ((1, 2),), jnp.float32)
    medium_rates = jnp.clip(jnp.exp(math.log(0.12) - 3.4011973 * jax.random.uniform(keys[6], (D,), jnp.float32) ** steps_of(keys[6], (D,), ((0, 2),), -0.2, 0.2)), 0.004, 0.12)
    return {"streams": streams, "doc_ids": doc_ids, "feat_short": feat_short, "filt_short": filt_short, "feat_medium": feat_medium, "filt_medium": filt_medium, "medium_rates": medium_rates}


def featurize(extended, taps_weight):
    widened = extended.astype(jnp.float32)
    return taps_weight[:, 0] * widened[2:] + taps_weight[:, 1] * widened[1:-1] + taps_weight[:, 2] * widened[:-2]

def causal_rows(product, filter_taps):
    widened = product.astype(jnp.float32)
    tap_total = filter_taps.shape[0]
    out_rows = widened.shape[0] - tap_total + 1

    def add_tap(index, total):
        tap_index = jnp.asarray(index).astype(jnp.int32)
        start = (tap_total - 1 - tap_index).astype(jnp.int32)
        piece = lax.dynamic_slice_in_dim(widened, start, out_rows, 0)
        weight_row = lax.dynamic_index_in_dim(filter_taps, tap_index, 0, keepdims=False)
        return total + weight_row[None, :] * piece
    initial = jnp.zeros((out_rows, widened.shape[1]), widened.dtype)
    return lax.fori_loop(0, tap_total, add_tap, initial)

def conv_block(extended, taps_weight, filter_taps):
    row_total = extended.shape[0] - 1 - filter_taps.shape[0]
    features = featurize(extended, taps_weight)
    product = (features[:, 1] * features[:, 2]).astype(jnp.bfloat16)
    mixed_rows = causal_rows(product, filter_taps)
    query_feat = features[-row_total:, 0]
    value_sum = extended[-row_total:, 2].astype(jnp.float32) + query_feat * mixed_rows
    return jnp.stack([query_feat, features[-row_total:, 1], value_sum], 1).astype(jnp.bfloat16)

def attend(packed, doc_ids, start_row, row_total):
    key_rows = packed[:, 1].astype(jnp.float32)
    value_rows = packed[:, 2].astype(jnp.float32)
    seq_total = packed.shape[0]
    head_count = packed.shape[2]
    head_depth = packed.shape[3]
    query_rows = lax.dynamic_slice_in_dim(packed[:, 0], start_row, row_total, 0)
    query_blocks = query_rows.reshape(row_total // QBLOCK, QBLOCK, head_count, head_depth)
    key_pos = jnp.arange(seq_total, dtype=jnp.int32)
    score_scale = 1.0 / math.sqrt(head_depth)

    def score_block(block_pair):
        query_block, first_row = block_pair
        scores = jnp.einsum('qhd,khd->hqk', query_block.astype(jnp.float32), key_rows) * score_scale
        query_pos = first_row + jnp.arange(QBLOCK, dtype=jnp.int32)
        query_doc = lax.dynamic_slice_in_dim(doc_ids, first_row, QBLOCK, 0)
        allowed = (key_pos[None, :] <= query_pos[:, None]) & (doc_ids[None, :] == query_doc[:, None])
        scores = jnp.where(allowed[None], scores, -1e+30)
        row_max = lax.optimization_barrier(jnp.max(scores, axis=2, keepdims=True))
        exponent = jnp.exp(scores - row_max)
        weights = (exponent / lax.optimization_barrier(jnp.sum(exponent, axis=2, keepdims=True))).astype(jnp.bfloat16)
        return jnp.einsum('hqk,khd->qhd', weights.astype(jnp.float32), value_rows).astype(jnp.bfloat16)
    first_rows = start_row + QBLOCK * jnp.arange(row_total // QBLOCK, dtype=jnp.int32)
    attended = lax.map(score_block, (query_blocks, first_rows))
    return attended.reshape(row_total, head_count, head_depth)

def reference(streams, doc_ids, feat_short, filt_short, feat_medium, filt_medium, medium_rates):
    first_entry = streams[0]
    second_entry = streams[1]
    taps = jnp.arange(MR_LEN, dtype=jnp.float32)
    medium_filter = filt_medium * jnp.exp(-medium_rates[None, :] * taps[:, None])
    short_pad = jnp.zeros((SE_LEN + 1, 3, D), jnp.bfloat16)
    short_out = conv_block(jnp.concatenate([short_pad, first_entry], 0), feat_short, filt_short)
    medium_pad = jnp.zeros((MR_LEN + 1, 3, D), jnp.bfloat16)
    conv_out = conv_block(jnp.concatenate([medium_pad, short_out], 0), feat_medium, medium_filter)
    by_head = jnp.moveaxis(second_entry.reshape(L, 3, HEADS, HEAD_DIM), 2, 0)[:, :, :, None, :]

    def one_head(head_streams):
        return attend(head_streams, doc_ids, 0, L)
    attended = lax.map(one_head, by_head)
    attended = jnp.moveaxis(attended[:, :, 0, :], 0, 1).reshape(L, D)
    value_sum = (second_entry[:, 2].astype(jnp.float32) + attended.astype(jnp.float32)).astype(jnp.bfloat16)
    attn_state = jnp.stack([second_entry[:, 0], second_entry[:, 1], value_sum], 1)
    return jnp.stack([attn_state, conv_out], 0)
```

```python
import functools
import math

import jax
import jax.numpy as jnp
from jax import lax
from jax.experimental import pallas as pl
from jax.experimental.pallas import tpu as pltpu
from jax.sharding import PartitionSpec as P

HEAD_DIM = 128
CHUNKS = 2
HALO = 16
LANES = 128


def shifted(array, axis, by):
    peers = lax.axis_size(axis)
    pairs = [(i, i + by) for i in range(peers) if 0 <= i + by < peers]
    return lax.ppermute(array, axis, pairs)


def swapped(array, axis):
    return lax.ppermute(array, axis, [(i, i ^ 1) for i in range(lax.axis_size(axis))])


def feature(rows, weight, stream, count):
    first = rows.shape[0] - count
    return (
        weight[stream, 0][None] * rows[first:]
        + weight[stream, 1][None] * rows[first - 1 : first - 1 + count]
        + weight[stream, 2][None] * rows[first - 2 : first - 2 + count]
    )


def short_kernel(halo_ref, x_ref, feat_ref, filt_ref, feat2_ref, out_ref, tail_ref):
    rows = x_ref.shape[1]
    taps = filt_ref.shape[0]
    weight = feat_ref[...]

    def wide(stream):
        return jnp.concatenate(
            [halo_ref[stream].astype(jnp.float32), x_ref[stream].astype(jnp.float32)], 0
        )

    count = rows + 8
    query = feature(wide(0), weight, 0, rows)
    key = feature(wide(1), weight, 1, count)
    value_rows = wide(2)
    value = feature(value_rows, weight, 2, count)
    product = (key * value).astype(jnp.bfloat16).astype(jnp.float32)
    mixed = filt_ref[0][None] * product[8:]
    for j in range(1, taps):
        mixed += filt_ref[j][None] * product[8 - j : 8 - j + rows]
    new_key = key[8:].astype(jnp.bfloat16)
    new_value = (x_ref[2].astype(jnp.float32) + query * mixed).astype(jnp.bfloat16)
    out_ref[0] = query.astype(jnp.bfloat16)
    out_ref[1] = new_key
    out_ref[2] = new_value
    tail = tail_ref.shape[0]
    weight2 = feat2_ref[...]
    tail_key = feature(new_key.astype(jnp.float32), weight2, 1, tail)
    tail_value = feature(new_value.astype(jnp.float32), weight2, 2, tail)
    tail_ref[...] = (tail_key * tail_value).astype(jnp.bfloat16)


def medium_kernel(halo_ref, past_ref, x_ref, feat_ref, filt_ref, rate_ref, out_ref, shift_ref, h_ref):
    rows = x_ref.shape[1]
    taps = filt_ref.shape[0]
    weight = feat_ref[...]

    def wide(stream):
        return jnp.concatenate(
            [halo_ref[stream].astype(jnp.float32), x_ref[stream].astype(jnp.float32)], 0
        )

    query = feature(wide(0), weight, 0, rows)
    key = feature(wide(1), weight, 1, rows)
    value = feature(wide(2), weight, 2, rows)
    out_ref[0] = query.astype(jnp.bfloat16)
    out_ref[1] = key.astype(jnp.bfloat16)
    product = (key * value).astype(jnp.bfloat16).astype(jnp.float32)
    shift_ref[0, :taps] = past_ref[...].astype(jnp.float32)
    shift_ref[0, taps:] = product
    length = taps + rows
    for r in range(1, 8):
        shift_ref[r, 8:] = shift_ref[0, 8 - r : length - r]
    position = lax.broadcasted_iota(jnp.int32, filt_ref.shape, 0).astype(jnp.float32)
    h_ref[...] = filt_ref[...] * jnp.exp(-rate_ref[...] * position)

    def step(m, total):
        weights = h_ref[pl.ds(pl.multiple_of(8 * m, 8), 8), :]
        start = pl.multiple_of(taps - 8 * m, 8)
        for r in range(8):
            total += weights[r : r + 1] * shift_ref[r, pl.ds(start, rows), :]
        return total

    mixed = lax.fori_loop(0, taps // 8, step, jnp.zeros((rows, x_ref.shape[2]), jnp.float32))
    out_ref[2] = (x_ref[2].astype(jnp.float32) + query * mixed).astype(jnp.bfloat16)


def short_block(halo, x, feat, filt, feat2, tail):
    _, rows, width = x.shape
    col3 = lambda n: pl.BlockSpec((3, n, LANES), lambda c: (0, 0, c))
    col2 = lambda n: pl.BlockSpec((n, LANES), lambda c: (0, c))
    return pl.pallas_call(
        short_kernel,
        grid=(width // LANES,),
        in_specs=[col3(HALO), col3(rows), col3(3), col2(filt.shape[0]), col3(3)],
        out_specs=[col3(rows), col2(tail)],
        out_shape=[
            jax.ShapeDtypeStruct((3, rows, width), jnp.bfloat16),
            jax.ShapeDtypeStruct((tail, width), jnp.bfloat16),
        ],
        cost_estimate=pl.CostEstimate(
            flops=60 * rows * width, bytes_accessed=12 * rows * width, transcendentals=0
        ),
    )(halo, x, feat, filt, feat2)


def medium_block(halo, past, x, feat, filt, rates):
    _, rows, width = x.shape
    taps = filt.shape[0]
    col3 = lambda n: pl.BlockSpec((3, n, LANES), lambda c: (0, 0, c))
    col2 = lambda n: pl.BlockSpec((n, LANES), lambda c: (0, c))
    return pl.pallas_call(
        medium_kernel,
        grid=(width // LANES,),
        in_specs=[col3(HALO), col2(taps), col3(rows), col3(3), col2(taps), col2(1)],
        out_specs=col3(rows),
        out_shape=jax.ShapeDtypeStruct((3, rows, width), jnp.bfloat16),
        scratch_shapes=[
            pltpu.VMEM((8, taps + rows, LANES), jnp.float32),
            pltpu.VMEM((taps, LANES), jnp.float32),
        ],
        cost_estimate=pl.CostEstimate(
            flops=300 * rows * width, bytes_accessed=14 * rows * width, transcendentals=0
        ),
    )(halo, past, x, feat, filt, rates[None])


def attention_kernel(hops, query_doc_ref, key_doc_ref, q_ref, *refs):
    blocks, out_ref, bias_ref = refs[: hops + 1], refs[hops + 1], refs[hops + 2]
    rows = q_ref.shape[1]
    keys = rows * (hops + 1)

    @pl.when(pl.program_id(0) == 0)
    def _():
        row = lax.broadcasted_iota(jnp.int32, (rows, keys), 0)
        column = lax.broadcasted_iota(jnp.int32, (rows, keys), 1)
        allowed = (column - rows * hops <= row) & (key_doc_ref[...] == query_doc_ref[...])
        bias_ref[...] = jnp.where(allowed, 0.0, -1e30)

    scale = 1.0 / math.sqrt(HEAD_DIM)
    key = jnp.concatenate([block[0] for block in blocks], 0)
    value = jnp.concatenate([block[1] for block in blocks], 0)
    scores = lax.dot_general(
        q_ref[0], key, (((1,), (1,)), ((), ())), preferred_element_type=jnp.float32
    )
    scores = scores * scale + bias_ref[...]
    exponent = jnp.exp(scores - jnp.max(scores, axis=1, keepdims=True))
    total = jnp.sum(exponent, axis=1, keepdims=True)
    attended = jnp.dot(exponent.astype(jnp.bfloat16), value, preferred_element_type=jnp.float32)
    attended = (attended / total).astype(jnp.bfloat16).astype(jnp.float32)
    out_ref[...] = (blocks[hops][1].astype(jnp.float32) + attended).astype(jnp.bfloat16)


def attention(query, blocks, query_doc, key_doc):
    hops = len(blocks) - 1
    _, rows, width = blocks[0].shape
    keys = rows * (hops + 1)
    heads = width // HEAD_DIM
    return pl.pallas_call(
        functools.partial(attention_kernel, hops),
        grid=(heads,),
        in_specs=[
            pl.BlockSpec((rows, 1), lambda h: (0, 0)),
            pl.BlockSpec((1, keys), lambda h: (0, 0)),
            pl.BlockSpec((1, rows, HEAD_DIM), lambda h: (0, 0, h)),
        ]
        + [pl.BlockSpec((2, rows, HEAD_DIM), lambda h: (0, 0, h))] * (hops + 1),
        out_specs=pl.BlockSpec((rows, HEAD_DIM), lambda h: (0, h)),
        out_shape=jax.ShapeDtypeStruct((rows, width), jnp.bfloat16),
        scratch_shapes=[pltpu.VMEM((rows, keys), jnp.float32)],
        cost_estimate=pl.CostEstimate(
            flops=4 * rows * keys * width,
            bytes_accessed=4 * keys * width,
            transcendentals=rows * keys * heads,
        ),
    )(query_doc, key_doc, query, *blocks)


def local(streams, doc_ids, feat_short, filt_short, feat_medium, filt_medium, medium_rates):
    rows = streams.shape[1]
    channels = streams.shape[3]
    half = channels // 2
    tail = filt_medium.shape[0]
    first = lax.axis_index("phase") == 0
    seq_total = rows * lax.axis_size("ctx")
    hops = -(-(seq_total // 2 - 1) // rows)
    start = lax.axis_index("ctx") * rows
    padded_doc = jnp.concatenate([jnp.full((hops * rows,), -1, jnp.int32), doc_ids], 0)
    key_doc = lax.dynamic_slice_in_dim(padded_doc, start, (hops + 1) * rows, 0)[None]
    query_doc = key_doc[0, hops * rows :][:, None]

    state = jnp.transpose(streams[0], (1, 0, 2))
    width = half // CHUNKS

    def part(array, chunk, mine):
        low = array[..., chunk * width : (chunk + 1) * width]
        high = array[..., half + chunk * width : half + (chunk + 1) * width]
        return jnp.where(first, high, low) if mine else jnp.where(first, low, high)

    swaps = [swapped(part(state, c, False), "phase") for c in range(CHUNKS)]
    lows, highs = [], []
    for c in range(CHUNKS):
        own = part(state, c, True)
        other = swaps[c]
        conv_in = jnp.where(first, own, other)
        attn_in = jnp.where(first, other, own)
        block = attn_in[1:]
        blocks = [block]
        for _ in range(hops):
            block = shifted(block, "ctx", 1)
            blocks.insert(0, block)

        halo = shifted(conv_in[:, rows - HALO :], "ctx", 1)
        feat2 = part(feat_medium, c, True)
        short_out, tail_product = short_block(
            halo, conv_in, part(feat_short, c, True), part(filt_short, c, True), feat2, tail
        )
        halo2 = shifted(short_out[:, rows - HALO :], "ctx", 1)
        past = shifted(tail_product, "ctx", 1)
        conv_out = medium_block(
            halo2,
            past,
            short_out,
            feat2,
            part(filt_medium, c, True),
            part(medium_rates, c, True),
        )
        got_pair = swapped(jnp.where(first, conv_out[:2], attn_in[:2]), "phase")
        value = attention(attn_in, blocks, query_doc, key_doc)
        got_value = swapped(jnp.where(first, conv_out[2], value), "phase")
        got = jnp.concatenate([got_pair, got_value[None]], 0)
        kept = jnp.where(first, jnp.concatenate([attn_in[:2], value[None]], 0), conv_out)
        lows.append(jnp.where(first, got, kept))
        highs.append(jnp.where(first, kept, got))
    out = jnp.concatenate(lows + highs, 2)
    return jnp.transpose(out, (1, 0, 2))[None]


def solution(mesh):
    in_specs = (
        P("phase", "ctx", None, "mp"),
        P(),
        P(None, None, "mp"),
        P(None, "mp"),
        P(None, None, "mp"),
        P(None, "mp"),
        P("mp"),
    )
    out_specs = P("phase", "ctx", None, "mp")
    return jax.shard_map(local, mesh=mesh, in_specs=in_specs, out_specs=out_specs, check_vma=False)
```

```python
import functools
import math

import jax
import jax.numpy as jnp
from jax import lax
from jax.experimental import pallas as pl
from jax.experimental.pallas import tpu as pltpu
from jax.sharding import PartitionSpec as P

HEAD_DIM = 128
CHUNKS = 4
HALO = 16
LANES = 128
MESH = pl.DeviceIdType.MESH


def feature(rows, weight, stream, count):
    first = rows.shape[0] - count
    return (
        weight[stream, 0][None] * rows[first:]
        + weight[stream, 1][None] * rows[first - 1 : first - 1 + count]
        + weight[stream, 2][None] * rows[first - 2 : first - 2 + count]
    )


def tick_kernel(
    hops,
    own_ref,
    other_ref,
    query_doc_ref,
    key_doc_ref,
    feat_ref,
    filt_ref,
    feat2_ref,
    filt2_ref,
    rate_ref,
    kept_ref,
    got_ref,
    state,
    chain,
    halo,
    halo2,
    past,
    short,
    tail,
    shift_ref,
    h_ref,
    bias_ref,
    local_sems,
    send_sems,
    recv_sems,
):
    rows = state.shape[2]
    half = state.shape[3]
    width = half // CHUNKS
    tiles = width // LANES
    taps = filt2_ref.shape[0]
    keys = rows * (hops + 1)
    phase = lax.axis_index("phase")
    place = lax.axis_index("ctx")
    peers = lax.axis_size("ctx")
    right = lax.rem(place + 1, peers)
    left = lax.rem(place + peers - 1, peers)
    partner = 1 - phase
    begin = place == 0

    load_own = pltpu.make_async_copy(own_ref, state.at[phase], local_sems.at[0])
    load_own.start()

    barrier = pltpu.get_barrier_semaphore()
    for target in ({"ctx": left}, {"ctx": right}, {"phase": partner}):
        pl.semaphore_signal(barrier, inc=1, device_id=target, device_id_type=MESH)
    pl.semaphore_wait(barrier, 3)

    def columns(chunk):
        return pl.ds(chunk * width, width)

    def remote(source, target, slot, device):
        return pltpu.make_async_remote_copy(
            src_ref=source,
            dst_ref=target,
            send_sem=send_sems.at[slot],
            recv_sem=recv_sems.at[slot],
            device_id=device,
            device_id_type=MESH,
        )

    per = hops + 6
    to_right = {"ctx": right}
    to_partner = {"phase": partner}

    def swap(c):
        return remote(
            other_ref.at[:, :, columns(c)], state.at[phase, :, :, columns(c)], c * per, to_partner
        )

    def hop(c, s):
        source = (
            state.at[1, pl.ds(1, 2), :, columns(c)]
            if s == 0
            else chain.at[s - 1, :, :, columns(c)]
        )
        return remote(source, chain.at[s, :, :, columns(c)], c * per + 6 + s, to_right)

    def send_halo(c):
        rows_ref = state.at[0, :, pl.ds(rows - HALO, HALO), columns(c)]
        return remote(rows_ref, halo.at[:, :, columns(c)], c * per + 1, to_right)

    def send_halo2(c):
        rows_ref = short.at[:, pl.ds(rows - HALO, HALO), columns(c)]
        return remote(rows_ref, halo2.at[:, :, columns(c)], c * per + 2, to_right)

    def send_past(c):
        return remote(tail.at[:, columns(c)], past.at[:, columns(c)], c * per + 3, to_right)

    def send_pair(c):
        return remote(
            state.at[phase, pl.ds(0, 2), :, columns(c)],
            got_ref.at[pl.ds(0, 2), :, columns(c)],
            c * per + 4,
            to_partner,
        )

    def send_value(c):
        return remote(
            state.at[phase, pl.ds(2, 1), :, columns(c)],
            got_ref.at[pl.ds(2, 1), :, columns(c)],
            c * per + 5,
            to_partner,
        )

    def keep(c):
        return pltpu.make_async_copy(
            state.at[partner, :, :, columns(c)], kept_ref.at[:, :, columns(c)], local_sems.at[1 + c]
        )

    for c in range(CHUNKS):
        swap(c).start()

    row = lax.broadcasted_iota(jnp.int32, (rows, keys), 0)
    column = lax.broadcasted_iota(jnp.int32, (rows, keys), 1)
    allowed = (column - rows * hops <= row) & (key_doc_ref[...] == query_doc_ref[...])
    bias_ref[...] = jnp.where(allowed, 0.0, -1e30)

    def over_tiles(chunk, body):
        def one(index, carry):
            body(pl.ds(pl.multiple_of(chunk * width + index * LANES, LANES), LANES))
            return carry

        lax.fori_loop(0, tiles, one, 0)

    def earlier(block):
        return jnp.where(begin, 0.0, block.astype(jnp.float32))

    def short_tile(col):
        weight = feat_ref[:, :, col]

        def wide(stream):
            return jnp.concatenate(
                [earlier(halo[stream, :, col]), state[0, stream, :, col].astype(jnp.float32)], 0
            )

        count = rows + 8
        query = feature(wide(0), weight, 0, rows)
        key = feature(wide(1), weight, 1, count)
        value = feature(wide(2), weight, 2, count)
        product = (key * value).astype(jnp.bfloat16).astype(jnp.float32)
        filt = filt_ref[:, col]
        mixed = filt[0][None] * product[8:]
        for j in range(1, filt_ref.shape[0]):
            mixed += filt[j][None] * product[8 - j : 8 - j + rows]
        new_key = key[8:].astype(jnp.bfloat16)
        new_value = (state[0, 2, :, col].astype(jnp.float32) + query * mixed).astype(jnp.bfloat16)
        short[0, :, col] = query.astype(jnp.bfloat16)
        short[1, :, col] = new_key
        short[2, :, col] = new_value
        weight2 = feat2_ref[:, :, col]
        tail_key = feature(new_key.astype(jnp.float32), weight2, 1, taps)
        tail_value = feature(new_value.astype(jnp.float32), weight2, 2, taps)
        tail[:, col] = (tail_key * tail_value).astype(jnp.bfloat16)

    def medium_tile(col):
        weight = feat2_ref[:, :, col]

        def wide(stream):
            return jnp.concatenate(
                [earlier(halo2[stream, :, col]), short[stream, :, col].astype(jnp.float32)], 0
            )

        query = feature(wide(0), weight, 0, rows)
        key = feature(wide(1), weight, 1, rows)
        value = feature(wide(2), weight, 2, rows)
        state[0, 0, :, col] = query.astype(jnp.bfloat16)
        state[0, 1, :, col] = key.astype(jnp.bfloat16)
        shift_ref[0, :taps] = earlier(past[:, col])
        shift_ref[0, taps:] = (key * value).astype(jnp.bfloat16).astype(jnp.float32)
        length = taps + rows
        for r in range(1, 8):
            shift_ref[r, 8:] = shift_ref[0, 8 - r : length - r]
        position = lax.broadcasted_iota(jnp.int32, (taps, LANES), 0).astype(jnp.float32)
        h_ref[...] = filt2_ref[:, col] * jnp.exp(-rate_ref[:, col] * position)

        def step(m, total):
            weights = h_ref[pl.ds(pl.multiple_of(8 * m, 8), 8), :]
            first = pl.multiple_of(taps - 8 * m, 8)
            for r in range(8):
                total += weights[r : r + 1] * shift_ref[r, pl.ds(first, rows), :]
            return total

        mixed = lax.fori_loop(0, taps // 8, step, jnp.zeros((rows, LANES), jnp.float32))
        total = short[2, :, col].astype(jnp.float32) + query * mixed
        state[0, 2, :, col] = total.astype(jnp.bfloat16)

    def attention_tile(col):
        scale = 1.0 / math.sqrt(HEAD_DIM)
        order = list(range(hops))[::-1]
        key = jnp.concatenate([chain[s, 0, :, col] for s in order] + [state[1, 1, :, col]], 0)
        value = jnp.concatenate([chain[s, 1, :, col] for s in order] + [state[1, 2, :, col]], 0)
        scores = lax.dot_general(
            state[1, 0, :, col], key, (((1,), (1,)), ((), ())), preferred_element_type=jnp.float32
        )
        scores = scores * scale + bias_ref[...]
        exponent = jnp.exp(scores - jnp.max(scores, axis=1, keepdims=True))
        total = jnp.sum(exponent, axis=1, keepdims=True)
        attended = jnp.dot(exponent.astype(jnp.bfloat16), value, preferred_element_type=jnp.float32)
        attended = (attended / total).astype(jnp.bfloat16).astype(jnp.float32)
        summed = state[1, 2, :, col].astype(jnp.float32) + attended
        state[1, 2, :, col] = summed.astype(jnp.bfloat16)

    load_own.wait()
    last = 2 * (CHUNKS - 1) + hops
    for slot in range(last + 2):
        for c in range(CHUNKS):
            age = slot - 2 * c
            if age == 0:
                swap(c).wait_recv()
                hop(c, 0).start()
                send_halo(c).start()
            if 1 <= age <= hops:
                hop(c, age - 1).wait_recv()
                if age < hops:
                    hop(c, age).start()
            if age == 3:
                send_pair(c).start()
            if age == hops + 1:
                send_value(c).start()
                keep(c).start()
        for c in range(CHUNKS):
            age = slot - 2 * c
            if age == 1:
                send_halo(c).wait_recv()
                over_tiles(c, short_tile)
                send_halo2(c).start()
                send_past(c).start()
        for c in range(CHUNKS):
            age = slot - 2 * c
            if age == hops:
                hop(c, 0).wait_send()
                over_tiles(c, attention_tile)
        for c in range(CHUNKS):
            age = slot - 2 * c
            if age == 2:
                send_halo2(c).wait_recv()
                send_past(c).wait_recv()
                send_halo(c).wait_send()
                over_tiles(c, medium_tile)

    for c in range(CHUNKS):
        swap(c).wait_send()
        send_halo2(c).wait_send()
        send_past(c).wait_send()
        for s in range(1, hops):
            hop(c, s).wait_send()
        keep(c).wait()
        send_pair(c).wait()
        send_value(c).wait()


def local(streams, doc_ids, feat_short, filt_short, feat_medium, filt_medium, medium_rates):
    rows = streams.shape[1]
    channels = streams.shape[3]
    half = channels // 2
    taps = filt_medium.shape[0]
    first = lax.axis_index("phase") == 0
    seq_total = rows * lax.axis_size("ctx")
    hops = -(-(seq_total // 2 - 1) // rows)
    keys = (hops + 1) * rows
    start = lax.axis_index("ctx") * rows
    padded_doc = jnp.concatenate([jnp.full((hops * rows,), -1, jnp.int32), doc_ids], 0)
    key_doc = lax.dynamic_slice_in_dim(padded_doc, start, keys, 0)[None]
    query_doc = key_doc[0, hops * rows :][:, None]

    def mine(array):
        return jnp.where(first, array[..., half:], array[..., :half])

    def theirs(array):
        return jnp.where(first, array[..., :half], array[..., half:])

    state = jnp.transpose(streams[0], (1, 0, 2))
    anywhere = pl.BlockSpec(memory_space=pl.ANY)
    inside = pl.BlockSpec(memory_space=pltpu.VMEM)
    shape = jax.ShapeDtypeStruct((3, rows, half), jnp.bfloat16)
    slots = CHUNKS * (hops + 6)
    kept, got = pl.pallas_call(
        functools.partial(tick_kernel, hops),
        in_specs=[anywhere] * 2 + [inside] * 7,
        out_specs=[anywhere] * 2,
        out_shape=[shape, shape],
        scratch_shapes=[
            pltpu.VMEM((2, 3, rows, half), jnp.bfloat16),
            pltpu.VMEM((hops, 2, rows, half), jnp.bfloat16),
            pltpu.VMEM((3, HALO, half), jnp.bfloat16),
            pltpu.VMEM((3, HALO, half), jnp.bfloat16),
            pltpu.VMEM((taps, half), jnp.bfloat16),
            pltpu.VMEM((3, rows, half), jnp.bfloat16),
            pltpu.VMEM((taps, half), jnp.bfloat16),
            pltpu.VMEM((8, taps + rows, LANES), jnp.float32),
            pltpu.VMEM((taps, LANES), jnp.float32),
            pltpu.VMEM((rows, keys), jnp.float32),
            pltpu.SemaphoreType.DMA((1 + CHUNKS,)),
            pltpu.SemaphoreType.DMA((slots,)),
            pltpu.SemaphoreType.DMA((slots,)),
        ],
        compiler_params=pltpu.CompilerParams(
            collective_id=0, has_side_effects=True, vmem_limit_bytes=62 * 1024 * 1024
        ),
    )(
        mine(state),
        theirs(state),
        query_doc,
        key_doc,
        mine(feat_short),
        mine(filt_short),
        mine(feat_medium),
        mine(filt_medium),
        mine(medium_rates)[None],
    )
    low = jnp.where(first, got, kept)
    high = jnp.where(first, kept, got)
    return jnp.transpose(jnp.concatenate([low, high], 2), (1, 0, 2))[None]


def solution(mesh):
    in_specs = (
        P("phase", "ctx", None, "mp"),
        P(),
        P(None, None, "mp"),
        P(None, "mp"),
        P(None, None, "mp"),
        P(None, "mp"),
        P("mp"),
    )
    out_specs = P("phase", "ctx", None, "mp")
    return jax.shard_map(local, mesh=mesh, in_specs=in_specs, out_specs=out_specs, check_vma=False)
```

```python
import functools
import math

import jax
import jax.numpy as jnp
from jax import lax
from jax.experimental import pallas as pl
from jax.experimental.pallas import tpu as pltpu
from jax.sharding import PartitionSpec as P

HEAD_DIM = 128
CHUNKS = 4
HALO = 16
LANES = 128
MESH = pl.DeviceIdType.MESH


def feature(rows, weight, stream, count):
    first = rows.shape[0] - count
    return (
        weight[stream, 0][None] * rows[first:]
        + weight[stream, 1][None] * rows[first - 1 : first - 1 + count]
        + weight[stream, 2][None] * rows[first - 2 : first - 2 + count]
    )


def tick_kernel(
    hops,
    whole_ref,
    key_doc_ref,
    feat_all,
    filt_all,
    feat2_all,
    filt2_all,
    rate_all,
    out_ref,
    feat_ref,
    filt_ref,
    feat2_ref,
    filt2_ref,
    rate_ref,
    state,
    chain,
    halo,
    halo2,
    past,
    short,
    tail,
    shift_ref,
    h_ref,
    bias_ref,
    local_sems,
    send_sems,
    recv_sems,
):
    rows = state.shape[2]
    half = state.shape[3]
    width = half // CHUNKS
    tiles = width // LANES
    taps = filt2_ref.shape[0]
    keys = rows * (hops + 1)
    phase = lax.axis_index("phase")
    place = lax.axis_index("ctx")
    peers = lax.axis_size("ctx")
    right = lax.rem(place + 1, peers)
    left = lax.rem(place + peers - 1, peers)
    partner = 1 - phase
    begin = place == 0

    mine = partner * half
    theirs = phase * half

    def piece(offset, size):
        return pl.ds(pl.multiple_of(offset, LANES), size)

    loads = [
        pltpu.make_async_copy(
            whole_ref.at[:, :, piece(mine, half)], state.at[phase], local_sems.at[CHUNKS]
        )
    ]
    pairs = (
        (feat_all.at[:, :, piece(mine, half)], feat_ref),
        (filt_all.at[:, piece(mine, half)], filt_ref),
        (feat2_all.at[:, :, piece(mine, half)], feat2_ref),
        (filt2_all.at[:, piece(mine, half)], filt2_ref),
        (rate_all.at[:, piece(mine, half)], rate_ref),
    )
    for index, (source, target) in enumerate(pairs):
        loads.append(pltpu.make_async_copy(source, target, local_sems.at[CHUNKS + 1 + index]))

    barrier = pltpu.get_barrier_semaphore()
    for target in ({"ctx": left}, {"ctx": right}, {"phase": partner}):
        pl.semaphore_signal(barrier, inc=1, device_id=target, device_id_type=MESH)
    pl.semaphore_wait(barrier, 3)

    def columns(chunk):
        return pl.ds(chunk * width, width)

    def remote(source, target, slot, device):
        return pltpu.make_async_remote_copy(
            src_ref=source,
            dst_ref=target,
            send_sem=send_sems.at[slot],
            recv_sem=recv_sems.at[slot],
            device_id=device,
            device_id_type=MESH,
        )

    per = hops + 6
    to_right = {"ctx": right}
    to_partner = {"phase": partner}

    def swap(c):
        return remote(
            whole_ref.at[:, :, piece(theirs + c * width, width)], state.at[phase, :, :, columns(c)], c * per, to_partner
        )

    def hop(c, s):
        source = (
            state.at[1, pl.ds(1, 2), :, columns(c)]
            if s == 0
            else chain.at[s - 1, :, :, columns(c)]
        )
        return remote(source, chain.at[s, :, :, columns(c)], c * per + 6 + s, to_right)

    def send_halo(c):
        rows_ref = state.at[0, :, pl.ds(rows - HALO, HALO), columns(c)]
        return remote(rows_ref, halo.at[:, :, columns(c)], c * per + 1, to_right)

    def send_halo2(c):
        rows_ref = short.at[:, pl.ds(rows - HALO, HALO), columns(c)]
        return remote(rows_ref, halo2.at[:, :, columns(c)], c * per + 2, to_right)

    def send_past(c):
        return remote(tail.at[:, columns(c)], past.at[:, columns(c)], c * per + 3, to_right)

    def send_pair(c):
        return remote(
            state.at[phase, pl.ds(0, 2), :, columns(c)],
            out_ref.at[pl.ds(0, 2), :, piece(mine + c * width, width)],
            c * per + 4,
            to_partner,
        )

    def send_value(c):
        return remote(
            state.at[phase, pl.ds(2, 1), :, columns(c)],
            out_ref.at[pl.ds(2, 1), :, piece(mine + c * width, width)],
            c * per + 5,
            to_partner,
        )

    def keep(c):
        return pltpu.make_async_copy(
            state.at[partner, :, :, columns(c)],
            out_ref.at[:, :, piece(mine + c * width, width)],
            local_sems.at[c],
        )

    for c in range(CHUNKS):
        swap(c).start()
    for load in loads:
        load.start()

    row = lax.broadcasted_iota(jnp.int32, (rows, keys), 0)
    column = lax.broadcasted_iota(jnp.int32, (rows, keys), 1)
    key_doc = key_doc_ref[...].astype(jnp.float32)
    across = lax.broadcasted_iota(jnp.int32, (rows, rows), 1)
    down = lax.broadcasted_iota(jnp.int32, (rows, rows), 0)
    query_doc = jnp.sum(
        jnp.where(across == down, key_doc[:, rows * hops :], 0.0), axis=1, keepdims=True
    )
    allowed = (column - rows * hops <= row) & (key_doc == query_doc)
    bias_ref[...] = jnp.where(allowed, 0.0, -1e30)

    def over_tiles(chunk, body):
        def one(index, carry):
            body(pl.ds(pl.multiple_of(chunk * width + index * LANES, LANES), LANES))
            return carry

        lax.fori_loop(0, tiles, one, 0)

    def earlier(block):
        return jnp.where(begin, 0.0, block.astype(jnp.float32))

    def short_tile(col):
        weight = feat_ref[:, :, col]

        def wide(stream):
            return jnp.concatenate(
                [earlier(halo[stream, :, col]), state[0, stream, :, col].astype(jnp.float32)], 0
            )

        count = rows + 8
        query = feature(wide(0), weight, 0, rows)
        key = feature(wide(1), weight, 1, count)
        value = feature(wide(2), weight, 2, count)
        product = (key * value).astype(jnp.bfloat16).astype(jnp.float32)
        filt = filt_ref[:, col]
        mixed = filt[0][None] * product[8:]
        for j in range(1, filt_ref.shape[0]):
            mixed += filt[j][None] * product[8 - j : 8 - j + rows]
        new_key = key[8:].astype(jnp.bfloat16)
        new_value = (state[0, 2, :, col].astype(jnp.float32) + query * mixed).astype(jnp.bfloat16)
        short[0, :, col] = query.astype(jnp.bfloat16)
        short[1, :, col] = new_key
        short[2, :, col] = new_value
        weight2 = feat2_ref[:, :, col]
        tail_key = feature(new_key.astype(jnp.float32), weight2, 1, taps)
        tail_value = feature(new_value.astype(jnp.float32), weight2, 2, taps)
        tail[:, col] = (tail_key * tail_value).astype(jnp.bfloat16)

    def medium_tile(col):
        weight = feat2_ref[:, :, col]

        def wide(stream):
            return jnp.concatenate(
                [earlier(halo2[stream, :, col]), short[stream, :, col].astype(jnp.float32)], 0
            )

        query = feature(wide(0), weight, 0, rows)
        key = feature(wide(1), weight, 1, rows)
        value = feature(wide(2), weight, 2, rows)
        state[0, 0, :, col] = query.astype(jnp.bfloat16)
        state[0, 1, :, col] = key.astype(jnp.bfloat16)
        shift_ref[0, :taps] = earlier(past[:, col])
        shift_ref[0, taps:] = (key * value).astype(jnp.bfloat16).astype(jnp.float32)
        length = taps + rows
        for r in range(1, 8):
            shift_ref[r, 8:] = shift_ref[0, 8 - r : length - r]
        position = lax.broadcasted_iota(jnp.int32, (taps, LANES), 0).astype(jnp.float32)
        h_ref[...] = filt2_ref[:, col] * jnp.exp(-rate_ref[:, col] * position)

        def step(m, total):
            weights = h_ref[pl.ds(pl.multiple_of(8 * m, 8), 8), :]
            first = pl.multiple_of(taps - 8 * m, 8)
            for r in range(8):
                total += weights[r : r + 1] * shift_ref[r, pl.ds(first, rows), :]
            return total

        mixed = lax.fori_loop(0, taps // 8, step, jnp.zeros((rows, LANES), jnp.float32))
        total = short[2, :, col].astype(jnp.float32) + query * mixed
        state[0, 2, :, col] = total.astype(jnp.bfloat16)

    def attention_tile(col):
        scale = 1.0 / math.sqrt(HEAD_DIM)
        order = list(range(hops))[::-1]
        key = jnp.concatenate([chain[s, 0, :, col] for s in order] + [state[1, 1, :, col]], 0)
        value = jnp.concatenate([chain[s, 1, :, col] for s in order] + [state[1, 2, :, col]], 0)
        scores = lax.dot_general(
            state[1, 0, :, col], key, (((1,), (1,)), ((), ())), preferred_element_type=jnp.float32
        )
        scores = scores * scale + bias_ref[...]
        exponent = jnp.exp(scores - jnp.max(scores, axis=1, keepdims=True))
        total = jnp.sum(exponent, axis=1, keepdims=True)
        attended = jnp.dot(exponent.astype(jnp.bfloat16), value, preferred_element_type=jnp.float32)
        attended = (attended / total).astype(jnp.bfloat16).astype(jnp.float32)
        summed = state[1, 2, :, col].astype(jnp.float32) + attended
        state[1, 2, :, col] = summed.astype(jnp.bfloat16)

    for load in loads:
        load.wait()
    last = 2 * (CHUNKS - 1) + hops
    for slot in range(last + 2):
        for c in range(CHUNKS):
            age = slot - 2 * c
            if age == 0:
                swap(c).wait_recv()
                hop(c, 0).start()
                send_halo(c).start()
            if 1 <= age <= hops:
                hop(c, age - 1).wait_recv()
                if age < hops:
                    hop(c, age).start()
            if age == 3:
                send_pair(c).start()
            if age == hops + 1:
                send_value(c).start()
                keep(c).start()
        for c in range(CHUNKS):
            age = slot - 2 * c
            if age == 1:
                send_halo(c).wait_recv()
                over_tiles(c, short_tile)
                send_halo2(c).start()
                send_past(c).start()
        for c in range(CHUNKS):
            age = slot - 2 * c
            if age == hops:
                hop(c, 0).wait_send()
                over_tiles(c, attention_tile)
        for c in range(CHUNKS):
            age = slot - 2 * c
            if age == 2:
                send_halo2(c).wait_recv()
                send_past(c).wait_recv()
                send_halo(c).wait_send()
                over_tiles(c, medium_tile)

    for c in range(CHUNKS):
        swap(c).wait_send()
        send_halo2(c).wait_send()
        send_past(c).wait_send()
        for s in range(1, hops):
            hop(c, s).wait_send()
        keep(c).wait()
        send_pair(c).wait()
        send_value(c).wait()


def local(streams, doc_ids, feat_short, filt_short, feat_medium, filt_medium, medium_rates):
    rows = streams.shape[1]
    channels = streams.shape[3]
    half = channels // 2
    taps = filt_medium.shape[0]
    seq_total = rows * lax.axis_size("ctx")
    hops = -(-(seq_total // 2 - 1) // rows)
    keys = (hops + 1) * rows
    start = lax.axis_index("ctx") * rows
    padded_doc = jnp.concatenate([jnp.full((hops * rows,), -1, jnp.int32), doc_ids], 0)
    key_doc = lax.dynamic_slice_in_dim(padded_doc, start, keys, 0)[None]
    state = jnp.transpose(streams[0], (1, 0, 2))
    anywhere = pl.BlockSpec(memory_space=pl.ANY)
    inside = pl.BlockSpec(memory_space=pltpu.VMEM)
    slots = CHUNKS * (hops + 6)
    out = pl.pallas_call(
        functools.partial(tick_kernel, hops),
        in_specs=[anywhere, inside] + [anywhere] * 5,
        out_specs=anywhere,
        out_shape=jax.ShapeDtypeStruct((3, rows, channels), jnp.bfloat16),
        scratch_shapes=[
            pltpu.VMEM((3, 3, half), jnp.float32),
            pltpu.VMEM((filt_short.shape[0], half), jnp.float32),
            pltpu.VMEM((3, 3, half), jnp.float32),
            pltpu.VMEM((taps, half), jnp.float32),
            pltpu.VMEM((1, half), jnp.float32),
            pltpu.VMEM((2, 3, rows, half), jnp.bfloat16),
            pltpu.VMEM((hops, 2, rows, half), jnp.bfloat16),
            pltpu.VMEM((3, HALO, half), jnp.bfloat16),
            pltpu.VMEM((3, HALO, half), jnp.bfloat16),
            pltpu.VMEM((taps, half), jnp.bfloat16),
            pltpu.VMEM((3, rows, half), jnp.bfloat16),
            pltpu.VMEM((taps, half), jnp.bfloat16),
            pltpu.VMEM((8, taps + rows, LANES), jnp.float32),
            pltpu.VMEM((taps, LANES), jnp.float32),
            pltpu.VMEM((rows, keys), jnp.float32),
            pltpu.SemaphoreType.DMA((CHUNKS + 6,)),
            pltpu.SemaphoreType.DMA((slots,)),
            pltpu.SemaphoreType.DMA((slots,)),
        ],
        compiler_params=pltpu.CompilerParams(
            collective_id=0, has_side_effects=True, vmem_limit_bytes=62 * 1024 * 1024
        ),
    )(
        state,
        key_doc,
        feat_short,
        filt_short,
        feat_medium,
        filt_medium,
        medium_rates[None],
    )
    return jnp.transpose(out, (1, 0, 2))[None]


def solution(mesh):
    in_specs = (
        P("phase", "ctx", None, "mp"),
        P(),
        P(None, None, "mp"),
        P(None, "mp"),
        P(None, None, "mp"),
        P(None, "mp"),
        P("mp"),
    )
    out_specs = P("phase", "ctx", None, "mp")
    return jax.shard_map(local, mesh=mesh, in_specs=in_specs, out_specs=out_specs, check_vma=False)
```

```python
import functools
import math

import jax
import jax.numpy as jnp
from jax import lax
from jax.experimental import pallas as pl
from jax.experimental.pallas import tpu as pltpu
from jax.sharding import PartitionSpec as P

HEAD_DIM = 128
CHUNKS = 4
HALO = 16
PIECES = 4
LANES = 128
MESH = pl.DeviceIdType.MESH


def feature(rows, weight, stream, count):
    first = rows.shape[0] - count
    return (
        weight[stream, 0][None] * rows[first:]
        + weight[stream, 1][None] * rows[first - 1 : first - 1 + count]
        + weight[stream, 2][None] * rows[first - 2 : first - 2 + count]
    )


def tick_kernel(
    hops,
    whole_ref,
    key_doc_ref,
    feat_all,
    filt_all,
    feat2_all,
    filt2_all,
    rate_all,
    out_ref,
    feat_ref,
    filt_ref,
    feat2_ref,
    filt2_ref,
    rate_ref,
    state,
    chain,
    halo,
    halo2,
    past,
    short,
    tail,
    shift_ref,
    h_ref,
    bias_ref,
    local_sems,
    send_sems,
    recv_sems,
):
    rows = state.shape[2]
    half = state.shape[3]
    width = half // CHUNKS
    tiles = width // LANES
    taps = filt2_ref.shape[0]
    keys = rows * (hops + 1)
    phase = lax.axis_index("phase")
    place = lax.axis_index("ctx")
    peers = lax.axis_size("ctx")
    right, left = place + 1, place - 1
    partner = 1 - phase
    has_left, has_right = place > 0, place < peers - 1

    mine = partner * half
    theirs = phase * half

    def piece(offset, size):
        return pl.ds(pl.multiple_of(offset, LANES), size)

    loads = [
        pltpu.make_async_copy(
            whole_ref.at[:, :, piece(mine, half)], state.at[phase], local_sems.at[CHUNKS]
        )
    ]
    pairs = (
        (feat_all.at[:, :, piece(mine, half)], feat_ref),
        (filt_all.at[:, piece(mine, half)], filt_ref),
        (feat2_all.at[:, :, piece(mine, half)], feat2_ref),
        (filt2_all.at[:, piece(mine, half)], filt2_ref),
        (rate_all.at[:, piece(mine, half)], rate_ref),
    )
    for index, (source, target) in enumerate(pairs):
        loads.append(pltpu.make_async_copy(source, target, local_sems.at[CHUNKS + 1 + index]))

    barrier = pltpu.get_barrier_semaphore()
    pl.semaphore_signal(barrier, inc=1, device_id={"phase": partner}, device_id_type=MESH)

    @pl.when(has_left)
    def _():
        pl.semaphore_signal(barrier, inc=1, device_id={"ctx": left}, device_id_type=MESH)

    @pl.when(has_right)
    def _():
        pl.semaphore_signal(barrier, inc=1, device_id={"ctx": right}, device_id_type=MESH)

    inner = (place + peers - 1) // peers + (peers - 1 - place + peers - 1) // peers
    pl.semaphore_wait(barrier, 1 + inner)

    def columns(chunk):
        return pl.ds(chunk * width, width)

    def remote(source, target, slot, device):
        return pltpu.make_async_remote_copy(
            src_ref=source,
            dst_ref=target,
            send_sem=send_sems.at[slot],
            recv_sem=recv_sems.at[slot],
            device_id=device,
            device_id_type=MESH,
        )

    per = hops + 6
    to_right = {"ctx": right}
    to_partner = {"phase": partner}

    def swap(c):
        return remote(
            whole_ref.at[:, :, piece(theirs + c * width, width)], state.at[phase, :, :, columns(c)], c * per, to_partner
        )

    def hop(c, s):
        source = (
            state.at[1, pl.ds(1, 2), :, columns(c)]
            if s == 0
            else chain.at[s - 1, :, :, columns(c)]
        )
        return remote(source, chain.at[s, :, :, columns(c)], c * per + 6 + s, to_right)

    def send_halo(c):
        rows_ref = state.at[0, :, pl.ds(rows - HALO, HALO), columns(c)]
        return remote(rows_ref, halo.at[:, :, columns(c)], c * per + 1, to_right)

    def send_halo2(c):
        rows_ref = short.at[:, pl.ds(rows - HALO, HALO), columns(c)]
        return remote(rows_ref, halo2.at[:, :, columns(c)], c * per + 2, to_right)

    def send_past(c):
        return remote(tail.at[:, columns(c)], past.at[:, columns(c)], c * per + 3, to_right)

    def send_pair(c):
        return remote(
            state.at[phase, pl.ds(0, 2), :, columns(c)],
            out_ref.at[pl.ds(0, 2), :, piece(mine + c * width, width)],
            c * per + 4,
            to_partner,
        )

    def send_value(c):
        return remote(
            state.at[phase, pl.ds(2, 1), :, columns(c)],
            out_ref.at[pl.ds(2, 1), :, piece(mine + c * width, width)],
            c * per + 5,
            to_partner,
        )

    def keep(c):
        return pltpu.make_async_copy(
            state.at[partner, :, :, columns(c)],
            out_ref.at[:, :, piece(mine + c * width, width)],
            local_sems.at[c],
        )

    for c in range(CHUNKS):
        swap(c).start()
    for load in loads:
        load.start()

    @pl.when(place == 0)
    def _():
        halo[...] = jnp.zeros_like(halo)
        halo2[...] = jnp.zeros_like(halo2)
        past[...] = jnp.zeros_like(past)

    for s in range(hops):

        @pl.when(place <= s)
        def _():
            chain[s] = jnp.zeros(chain.shape[1:], chain.dtype)

    def start(condition, *copies):
        @pl.when(condition)
        def _():
            for copy in copies:
                copy.start()

    def sent(condition, *copies):
        @pl.when(condition)
        def _():
            for copy in copies:
                copy.wait_send()

    def arrived(condition, *copies):
        @pl.when(condition)
        def _():
            for copy in copies:
                copy.wait_recv()

    def sends_hop(s):
        return has_right & (place >= s)

    row = lax.broadcasted_iota(jnp.int32, (rows, keys), 0)
    column = lax.broadcasted_iota(jnp.int32, (rows, keys), 1)
    key_doc = key_doc_ref[...].astype(jnp.float32)
    across = lax.broadcasted_iota(jnp.int32, (rows, rows), 1)
    down = lax.broadcasted_iota(jnp.int32, (rows, rows), 0)
    query_doc = jnp.sum(
        jnp.where(across == down, key_doc[:, rows * hops :], 0.0), axis=1, keepdims=True
    )
    allowed = (column - rows * hops <= row) & (key_doc == query_doc)
    bias_ref[...] = jnp.where(allowed, 0.0, -1e30)

    def over_tiles(chunk, body):
        def one(index, carry):
            body(pl.ds(pl.multiple_of(chunk * width + index * LANES, LANES), LANES))
            return carry

        lax.fori_loop(0, tiles, one, 0)

    def earlier(block):
        return block.astype(jnp.float32)

    def short_tile(col):
        weight = feat_ref[:, :, col]

        def wide(stream):
            return jnp.concatenate(
                [earlier(halo[stream, :, col]), state[0, stream, :, col].astype(jnp.float32)], 0
            )

        count = rows + 8
        query = feature(wide(0), weight, 0, rows)
        key = feature(wide(1), weight, 1, count)
        value = feature(wide(2), weight, 2, count)
        product = (key * value).astype(jnp.bfloat16).astype(jnp.float32)
        filt = filt_ref[:, col]
        mixed = filt[0][None] * product[8:]
        for j in range(1, filt_ref.shape[0]):
            mixed += filt[j][None] * product[8 - j : 8 - j + rows]
        new_key = key[8:].astype(jnp.bfloat16)
        new_value = (state[0, 2, :, col].astype(jnp.float32) + query * mixed).astype(jnp.bfloat16)
        short[0, :, col] = query.astype(jnp.bfloat16)
        short[1, :, col] = new_key
        short[2, :, col] = new_value
        weight2 = feat2_ref[:, :, col]
        tail_key = feature(new_key.astype(jnp.float32), weight2, 1, taps)
        tail_value = feature(new_value.astype(jnp.float32), weight2, 2, taps)
        tail[:, col] = (tail_key * tail_value).astype(jnp.bfloat16)

    def medium_tile(col):
        weight = feat2_ref[:, :, col]

        def wide(stream):
            return jnp.concatenate(
                [earlier(halo2[stream, :, col]), short[stream, :, col].astype(jnp.float32)], 0
            )

        query = feature(wide(0), weight, 0, rows)
        key = feature(wide(1), weight, 1, rows)
        value = feature(wide(2), weight, 2, rows)
        state[0, 0, :, col] = query.astype(jnp.bfloat16)
        state[0, 1, :, col] = key.astype(jnp.bfloat16)
        shift_ref[0, :taps] = earlier(past[:, col])
        shift_ref[0, taps:] = (key * value).astype(jnp.bfloat16).astype(jnp.float32)
        length = taps + rows
        for r in range(1, 8):
            shift_ref[r, 8:] = shift_ref[0, 8 - r : length - r]
        position = lax.broadcasted_iota(jnp.int32, (taps, LANES), 0).astype(jnp.float32)
        h_ref[...] = filt2_ref[:, col] * jnp.exp(-rate_ref[:, col] * position)

        def step(m, total):
            weights = h_ref[pl.ds(pl.multiple_of(8 * m, 8), 8), :]
            first = pl.multiple_of(taps - 8 * m, 8)
            for r in range(8):
                total += weights[r : r + 1] * shift_ref[r, pl.ds(first, rows), :]
            return total

        mixed = lax.fori_loop(0, taps // 8, step, jnp.zeros((rows, LANES), jnp.float32))
        total = short[2, :, col].astype(jnp.float32) + query * mixed
        state[0, 2, :, col] = total.astype(jnp.bfloat16)

    def attention_tile(col):
        scale = 1.0 / math.sqrt(HEAD_DIM)
        order = list(range(hops))[::-1]
        key = jnp.concatenate([chain[s, 0, :, col] for s in order] + [state[1, 1, :, col]], 0)
        value = jnp.concatenate([chain[s, 1, :, col] for s in order] + [state[1, 2, :, col]], 0)
        scores = lax.dot_general(
            state[1, 0, :, col], key, (((1,), (1,)), ((), ())), preferred_element_type=jnp.float32
        )
        scores = scores * scale + bias_ref[...]
        exponent = jnp.exp(scores - jnp.max(scores, axis=1, keepdims=True))
        total = jnp.sum(exponent, axis=1, keepdims=True)
        attended = jnp.dot(exponent.astype(jnp.bfloat16), value, preferred_element_type=jnp.float32)
        attended = (attended / total).astype(jnp.bfloat16).astype(jnp.float32)
        summed = state[1, 2, :, col].astype(jnp.float32) + attended
        state[1, 2, :, col] = summed.astype(jnp.bfloat16)

    for load in loads:
        load.wait()
    last = 2 * (CHUNKS - 1) + hops
    for slot in range(last + 2):
        for c in range(CHUNKS):
            age = slot - 2 * c
            if age == 0:
                swap(c).wait_recv()
                start(has_right, hop(c, 0), send_halo(c))
            if 1 <= age <= hops:
                arrived(place >= age, hop(c, age - 1))
                if age < hops:
                    start(sends_hop(age), hop(c, age))
            if age == 3:
                send_pair(c).start()
            if age == hops + 1:
                send_value(c).start()
                keep(c).start()
        for c in range(CHUNKS):
            age = slot - 2 * c
            if age == 1:
                arrived(has_left, send_halo(c))
                over_tiles(c, short_tile)
                start(has_right, send_halo2(c), send_past(c))
        for c in range(CHUNKS):
            age = slot - 2 * c
            if age == hops:
                sent(has_right, hop(c, 0))
                over_tiles(c, attention_tile)
        for c in range(CHUNKS):
            age = slot - 2 * c
            if age == 2:
                arrived(has_left, send_halo2(c), send_past(c))
                sent(has_right, send_halo(c))
                over_tiles(c, medium_tile)

    for c in range(CHUNKS):
        swap(c).wait_send()
        sent(has_right, send_halo2(c), send_past(c))
        for s in range(1, hops):
            sent(sends_hop(s), hop(c, s))
        keep(c).wait()
        send_pair(c).wait()
        send_value(c).wait()


def copy_kernel(source, target, held, in_sems, out_sems):
    streams, rows, _ = source.shape
    size = rows // PIECES
    parts = [(i, pl.ds(j * size, size)) for i in range(streams) for j in range(PIECES)]
    ins = [
        pltpu.make_async_copy(source.at[part], held.at[part], in_sems.at[n])
        for n, part in enumerate(parts)
    ]
    outs = [
        pltpu.make_async_copy(held.at[part], target.at[part], out_sems.at[n])
        for n, part in enumerate(parts)
    ]
    for copy in ins:
        copy.start()
    for first, second in zip(ins, outs):
        first.wait()
        second.start()
    for copy in outs:
        copy.wait()


def copied(array):
    anywhere = pl.BlockSpec(memory_space=pl.ANY)
    count = array.shape[0] * PIECES
    return pl.pallas_call(
        copy_kernel,
        in_specs=[anywhere],
        out_specs=anywhere,
        out_shape=jax.ShapeDtypeStruct(array.shape, array.dtype),
        scratch_shapes=[
            pltpu.VMEM(array.shape, array.dtype),
            pltpu.SemaphoreType.DMA((count,)),
            pltpu.SemaphoreType.DMA((count,)),
        ],
    )(array)


def local(streams, doc_ids, feat_short, filt_short, feat_medium, filt_medium, medium_rates):
    rows = streams.shape[1]
    channels = streams.shape[3]
    half = channels // 2
    taps = filt_medium.shape[0]
    seq_total = rows * lax.axis_size("ctx")
    hops = -(-(seq_total // 2 - 1) // rows)
    keys = (hops + 1) * rows
    start = lax.axis_index("ctx") * rows
    padded_doc = jnp.concatenate([jnp.full((hops * rows,), -1, jnp.int32), doc_ids], 0)
    key_doc = lax.dynamic_slice_in_dim(padded_doc, start, keys, 0)[None]
    state = jnp.transpose(streams[0], (1, 0, 2))
    anywhere = pl.BlockSpec(memory_space=pl.ANY)
    inside = pl.BlockSpec(memory_space=pltpu.VMEM)
    slots = CHUNKS * (hops + 6)
    out = pl.pallas_call(
        functools.partial(tick_kernel, hops),
        in_specs=[anywhere, inside] + [anywhere] * 5,
        out_specs=anywhere,
        out_shape=jax.ShapeDtypeStruct((3, rows, channels), jnp.bfloat16),
        scratch_shapes=[
            pltpu.VMEM((3, 3, half), jnp.float32),
            pltpu.VMEM((filt_short.shape[0], half), jnp.float32),
            pltpu.VMEM((3, 3, half), jnp.float32),
            pltpu.VMEM((taps, half), jnp.float32),
            pltpu.VMEM((1, half), jnp.float32),
            pltpu.VMEM((2, 3, rows, half), jnp.bfloat16),
            pltpu.VMEM((hops, 2, rows, half), jnp.bfloat16),
            pltpu.VMEM((3, HALO, half), jnp.bfloat16),
            pltpu.VMEM((3, HALO, half), jnp.bfloat16),
            pltpu.VMEM((taps, half), jnp.bfloat16),
            pltpu.VMEM((3, rows, half), jnp.bfloat16),
            pltpu.VMEM((taps, half), jnp.bfloat16),
            pltpu.VMEM((8, taps + rows, LANES), jnp.float32),
            pltpu.VMEM((taps, LANES), jnp.float32),
            pltpu.VMEM((rows, keys), jnp.float32),
            pltpu.SemaphoreType.DMA((CHUNKS + 6,)),
            pltpu.SemaphoreType.DMA((slots,)),
            pltpu.SemaphoreType.DMA((slots,)),
        ],
        compiler_params=pltpu.CompilerParams(
            collective_id=0, has_side_effects=True, vmem_limit_bytes=62 * 1024 * 1024
        ),
    )(
        state,
        key_doc,
        feat_short,
        filt_short,
        feat_medium,
        filt_medium,
        medium_rates[None],
    )
    return jnp.transpose(copied(out), (1, 0, 2))[None]


def solution(mesh):
    in_specs = (
        P("phase", "ctx", None, "mp"),
        P(),
        P(None, None, "mp"),
        P(None, "mp"),
        P(None, None, "mp"),
        P(None, "mp"),
        P("mp"),
    )
    out_specs = P("phase", "ctx", None, "mp")
    return jax.shard_map(local, mesh=mesh, in_specs=in_specs, out_specs=out_specs, check_vma=False)
```

```python
import functools
import math

import jax
import jax.numpy as jnp
from jax import lax
from jax.experimental import pallas as pl
from jax.experimental.pallas import tpu as pltpu
from jax.sharding import PartitionSpec as P

HEAD_DIM = 128
CHUNKS = 8
HALO = 16
PIECES = 4
LANES = 128
MESH = pl.DeviceIdType.MESH


def feature(rows, weight, stream, count):
    first = rows.shape[0] - count
    return (
        weight[stream, 0][None] * rows[first:]
        + weight[stream, 1][None] * rows[first - 1 : first - 1 + count]
        + weight[stream, 2][None] * rows[first - 2 : first - 2 + count]
    )


def tick_kernel(
    hops,
    whole_ref,
    key_doc_ref,
    feat_all,
    filt_all,
    feat2_all,
    filt2_all,
    rate_all,
    out_ref,
    feat_ref,
    filt_ref,
    feat2_ref,
    filt2_ref,
    rate_ref,
    state,
    chain,
    halo,
    halo2,
    past,
    short,
    tail,
    shift_ref,
    h_ref,
    bias_ref,
    local_sems,
    send_sems,
    recv_sems,
):
    rows = state.shape[2]
    half = state.shape[3]
    width = half // CHUNKS
    tiles = width // LANES
    taps = filt2_ref.shape[0]
    keys = rows * (hops + 1)
    phase = lax.axis_index("phase")
    place = lax.axis_index("ctx")
    peers = lax.axis_size("ctx")
    right, left = place + 1, place - 1
    partner = 1 - phase
    has_left, has_right = place > 0, place < peers - 1

    mine = partner * half
    theirs = phase * half

    def piece(offset, size):
        return pl.ds(pl.multiple_of(offset, LANES), size)

    loads = [
        pltpu.make_async_copy(
            whole_ref.at[:, :, piece(mine, half)], state.at[phase], local_sems.at[CHUNKS]
        )
    ]
    pairs = (
        (feat_all.at[:, :, piece(mine, half)], feat_ref),
        (filt_all.at[:, piece(mine, half)], filt_ref),
        (feat2_all.at[:, :, piece(mine, half)], feat2_ref),
        (filt2_all.at[:, piece(mine, half)], filt2_ref),
        (rate_all.at[:, piece(mine, half)], rate_ref),
    )
    for index, (source, target) in enumerate(pairs):
        loads.append(pltpu.make_async_copy(source, target, local_sems.at[CHUNKS + 1 + index]))

    barrier = pltpu.get_barrier_semaphore()
    pl.semaphore_signal(barrier, inc=1, device_id={"phase": partner}, device_id_type=MESH)

    @pl.when(has_left)
    def _():
        pl.semaphore_signal(barrier, inc=1, device_id={"ctx": left}, device_id_type=MESH)

    @pl.when(has_right)
    def _():
        pl.semaphore_signal(barrier, inc=1, device_id={"ctx": right}, device_id_type=MESH)

    inner = (place + peers - 1) // peers + (peers - 1 - place + peers - 1) // peers
    pl.semaphore_wait(barrier, 1 + inner)

    def columns(chunk):
        return pl.ds(chunk * width, width)

    def remote(source, target, slot, device):
        return pltpu.make_async_remote_copy(
            src_ref=source,
            dst_ref=target,
            send_sem=send_sems.at[slot],
            recv_sem=recv_sems.at[slot],
            device_id=device,
            device_id_type=MESH,
        )

    per = hops + 6
    to_right = {"ctx": right}
    to_partner = {"phase": partner}

    def swap(c):
        return remote(
            whole_ref.at[:, :, piece(theirs + c * width, width)], state.at[phase, :, :, columns(c)], c * per, to_partner
        )

    def hop(c, s):
        source = (
            state.at[1, pl.ds(1, 2), :, columns(c)]
            if s == 0
            else chain.at[s - 1, :, :, columns(c)]
        )
        return remote(source, chain.at[s, :, :, columns(c)], c * per + 6 + s, to_right)

    def send_halo(c):
        rows_ref = state.at[0, :, pl.ds(rows - HALO, HALO), columns(c)]
        return remote(rows_ref, halo.at[:, :, columns(c)], c * per + 1, to_right)

    def send_halo2(c):
        rows_ref = short.at[:, pl.ds(rows - HALO, HALO), columns(c)]
        return remote(rows_ref, halo2.at[:, :, columns(c)], c * per + 2, to_right)

    def send_past(c):
        return remote(tail.at[:, columns(c)], past.at[:, columns(c)], c * per + 3, to_right)

    def send_pair(c):
        return remote(
            state.at[phase, pl.ds(0, 2), :, columns(c)],
            out_ref.at[pl.ds(0, 2), :, piece(mine + c * width, width)],
            c * per + 4,
            to_partner,
        )

    def send_value(c):
        return remote(
            state.at[phase, pl.ds(2, 1), :, columns(c)],
            out_ref.at[pl.ds(2, 1), :, piece(mine + c * width, width)],
            c * per + 5,
            to_partner,
        )

    def keep(c):
        return pltpu.make_async_copy(
            state.at[partner, :, :, columns(c)],
            out_ref.at[:, :, piece(mine + c * width, width)],
            local_sems.at[c],
        )

    for c in range(CHUNKS):
        swap(c).start()
    for load in loads:
        load.start()

    @pl.when(place == 0)
    def _():
        halo[...] = jnp.zeros_like(halo)
        halo2[...] = jnp.zeros_like(halo2)
        past[...] = jnp.zeros_like(past)

    for s in range(hops):

        @pl.when(place <= s)
        def _():
            chain[s] = jnp.zeros(chain.shape[1:], chain.dtype)

    def start(condition, *copies):
        @pl.when(condition)
        def _():
            for copy in copies:
                copy.start()

    def sent(condition, *copies):
        @pl.when(condition)
        def _():
            for copy in copies:
                copy.wait_send()

    def arrived(condition, *copies):
        @pl.when(condition)
        def _():
            for copy in copies:
                copy.wait_recv()

    def sends_hop(s):
        return has_right & (place >= s)

    row = lax.broadcasted_iota(jnp.int32, (rows, keys), 0)
    column = lax.broadcasted_iota(jnp.int32, (rows, keys), 1)
    key_doc = key_doc_ref[...].astype(jnp.float32)
    across = lax.broadcasted_iota(jnp.int32, (rows, rows), 1)
    down = lax.broadcasted_iota(jnp.int32, (rows, rows), 0)
    query_doc = jnp.sum(
        jnp.where(across == down, key_doc[:, rows * hops :], 0.0), axis=1, keepdims=True
    )
    allowed = (column - rows * hops <= row) & (key_doc == query_doc)
    bias_ref[...] = jnp.where(allowed, 0.0, -1e30)

    def over_tiles(chunk, body):
        def one(index, carry):
            body(pl.ds(pl.multiple_of(chunk * width + index * LANES, LANES), LANES))
            return carry

        lax.fori_loop(0, tiles, one, 0)

    def earlier(block):
        return block.astype(jnp.float32)

    def short_tile(col):
        weight = feat_ref[:, :, col]

        def wide(stream):
            return jnp.concatenate(
                [earlier(halo[stream, :, col]), state[0, stream, :, col].astype(jnp.float32)], 0
            )

        count = rows + 8
        query = feature(wide(0), weight, 0, rows)
        key = feature(wide(1), weight, 1, count)
        value = feature(wide(2), weight, 2, count)
        product = (key * value).astype(jnp.bfloat16).astype(jnp.float32)
        filt = filt_ref[:, col]
        mixed = filt[0][None] * product[8:]
        for j in range(1, filt_ref.shape[0]):
            mixed += filt[j][None] * product[8 - j : 8 - j + rows]
        new_key = key[8:].astype(jnp.bfloat16)
        new_value = (state[0, 2, :, col].astype(jnp.float32) + query * mixed).astype(jnp.bfloat16)
        short[0, :, col] = query.astype(jnp.bfloat16)
        short[1, :, col] = new_key
        short[2, :, col] = new_value
        weight2 = feat2_ref[:, :, col]
        tail_key = feature(new_key.astype(jnp.float32), weight2, 1, taps)
        tail_value = feature(new_value.astype(jnp.float32), weight2, 2, taps)
        tail[:, col] = (tail_key * tail_value).astype(jnp.bfloat16)

    def medium_tile(col):
        weight = feat2_ref[:, :, col]

        def wide(stream):
            return jnp.concatenate(
                [earlier(halo2[stream, :, col]), short[stream, :, col].astype(jnp.float32)], 0
            )

        query = feature(wide(0), weight, 0, rows)
        key = feature(wide(1), weight, 1, rows)
        value = feature(wide(2), weight, 2, rows)
        state[0, 0, :, col] = query.astype(jnp.bfloat16)
        state[0, 1, :, col] = key.astype(jnp.bfloat16)
        shift_ref[0, :taps] = earlier(past[:, col])
        shift_ref[0, taps:] = (key * value).astype(jnp.bfloat16).astype(jnp.float32)
        length = taps + rows
        for r in range(1, 8):
            shift_ref[r, 8:] = shift_ref[0, 8 - r : length - r]
        position = lax.broadcasted_iota(jnp.int32, (taps, LANES), 0).astype(jnp.float32)
        h_ref[...] = filt2_ref[:, col] * jnp.exp(-rate_ref[:, col] * position)

        def step(m, total):
            weights = h_ref[pl.ds(pl.multiple_of(8 * m, 8), 8), :]
            first = pl.multiple_of(taps - 8 * m, 8)
            for r in range(8):
                total += weights[r : r + 1] * shift_ref[r, pl.ds(first, rows), :]
            return total

        mixed = lax.fori_loop(0, taps // 8, step, jnp.zeros((rows, LANES), jnp.float32))
        total = short[2, :, col].astype(jnp.float32) + query * mixed
        state[0, 2, :, col] = total.astype(jnp.bfloat16)

    def attention_tile(col):
        scale = 1.0 / math.sqrt(HEAD_DIM)
        order = list(range(hops))[::-1]
        key = jnp.concatenate([chain[s, 0, :, col] for s in order] + [state[1, 1, :, col]], 0)
        value = jnp.concatenate([chain[s, 1, :, col] for s in order] + [state[1, 2, :, col]], 0)
        scores = lax.dot_general(
            state[1, 0, :, col], key, (((1,), (1,)), ((), ())), preferred_element_type=jnp.float32
        )
        scores = scores * scale + bias_ref[...]
        exponent = jnp.exp(scores - jnp.max(scores, axis=1, keepdims=True))
        total = jnp.sum(exponent, axis=1, keepdims=True)
        attended = jnp.dot(exponent.astype(jnp.bfloat16), value, preferred_element_type=jnp.float32)
        attended = (attended / total).astype(jnp.bfloat16).astype(jnp.float32)
        summed = state[1, 2, :, col].astype(jnp.float32) + attended
        state[1, 2, :, col] = summed.astype(jnp.bfloat16)

    for load in loads:
        load.wait()
    last = 2 * (CHUNKS - 1) + hops
    for slot in range(last + 2):
        for c in range(CHUNKS):
            age = slot - 2 * c
            if age == 0:
                swap(c).wait_recv()
                start(has_right, hop(c, 0), send_halo(c))
            if 1 <= age <= hops:
                arrived(place >= age, hop(c, age - 1))
                if age < hops:
                    start(sends_hop(age), hop(c, age))
            if age == 3:
                send_pair(c).start()
            if age == hops + 1:
                send_value(c).start()
                keep(c).start()
        for c in range(CHUNKS):
            age = slot - 2 * c
            if age == 1:
                arrived(has_left, send_halo(c))
                over_tiles(c, short_tile)
                start(has_right, send_halo2(c), send_past(c))
        for c in range(CHUNKS):
            age = slot - 2 * c
            if age == hops:
                sent(has_right, hop(c, 0))
                over_tiles(c, attention_tile)
        for c in range(CHUNKS):
            age = slot - 2 * c
            if age == 2:
                arrived(has_left, send_halo2(c), send_past(c))
                sent(has_right, send_halo(c))
                over_tiles(c, medium_tile)

    for c in range(CHUNKS):
        swap(c).wait_send()
        sent(has_right, send_halo2(c), send_past(c))
        for s in range(1, hops):
            sent(sends_hop(s), hop(c, s))
        keep(c).wait()
        send_pair(c).wait()
        send_value(c).wait()


def copy_kernel(source, target, held, in_sems, out_sems):
    streams, rows, _ = source.shape
    size = rows // PIECES
    parts = [(i, pl.ds(j * size, size)) for i in range(streams) for j in range(PIECES)]
    ins = [
        pltpu.make_async_copy(source.at[part], held.at[part], in_sems.at[n])
        for n, part in enumerate(parts)
    ]
    outs = [
        pltpu.make_async_copy(held.at[part], target.at[part], out_sems.at[n])
        for n, part in enumerate(parts)
    ]
    for copy in ins:
        copy.start()
    for first, second in zip(ins, outs):
        first.wait()
        second.start()
    for copy in outs:
        copy.wait()


def copied(array):
    anywhere = pl.BlockSpec(memory_space=pl.ANY)
    count = array.shape[0] * PIECES
    return pl.pallas_call(
        copy_kernel,
        in_specs=[anywhere],
        out_specs=anywhere,
        out_shape=jax.ShapeDtypeStruct(array.shape, array.dtype),
        scratch_shapes=[
            pltpu.VMEM(array.shape, array.dtype),
            pltpu.SemaphoreType.DMA((count,)),
            pltpu.SemaphoreType.DMA((count,)),
        ],
    )(array)


def local(streams, doc_ids, feat_short, filt_short, feat_medium, filt_medium, medium_rates):
    rows = streams.shape[1]
    channels = streams.shape[3]
    half = channels // 2
    taps = filt_medium.shape[0]
    seq_total = rows * lax.axis_size("ctx")
    hops = -(-(seq_total // 2 - 1) // rows)
    keys = (hops + 1) * rows
    start = lax.axis_index("ctx") * rows
    padded_doc = jnp.concatenate([jnp.full((hops * rows,), -1, jnp.int32), doc_ids], 0)
    key_doc = lax.dynamic_slice_in_dim(padded_doc, start, keys, 0)[None]
    state = jnp.transpose(streams[0], (1, 0, 2))
    anywhere = pl.BlockSpec(memory_space=pl.ANY)
    inside = pl.BlockSpec(memory_space=pltpu.VMEM)
    slots = CHUNKS * (hops + 6)
    out = pl.pallas_call(
        functools.partial(tick_kernel, hops),
        in_specs=[anywhere, inside] + [anywhere] * 5,
        out_specs=anywhere,
        out_shape=jax.ShapeDtypeStruct((3, rows, channels), jnp.bfloat16),
        scratch_shapes=[
            pltpu.VMEM((3, 3, half), jnp.float32),
            pltpu.VMEM((filt_short.shape[0], half), jnp.float32),
            pltpu.VMEM((3, 3, half), jnp.float32),
            pltpu.VMEM((taps, half), jnp.float32),
            pltpu.VMEM((1, half), jnp.float32),
            pltpu.VMEM((2, 3, rows, half), jnp.bfloat16),
            pltpu.VMEM((hops, 2, rows, half), jnp.bfloat16),
            pltpu.VMEM((3, HALO, half), jnp.bfloat16),
            pltpu.VMEM((3, HALO, half), jnp.bfloat16),
            pltpu.VMEM((taps, half), jnp.bfloat16),
            pltpu.VMEM((3, rows, half), jnp.bfloat16),
            pltpu.VMEM((taps, half), jnp.bfloat16),
            pltpu.VMEM((8, taps + rows, LANES), jnp.float32),
            pltpu.VMEM((taps, LANES), jnp.float32),
            pltpu.VMEM((rows, keys), jnp.float32),
            pltpu.SemaphoreType.DMA((CHUNKS + 6,)),
            pltpu.SemaphoreType.DMA((slots,)),
            pltpu.SemaphoreType.DMA((slots,)),
        ],
        compiler_params=pltpu.CompilerParams(
            collective_id=0, has_side_effects=True, vmem_limit_bytes=62 * 1024 * 1024
        ),
    )(
        state,
        key_doc,
        feat_short,
        filt_short,
        feat_medium,
        filt_medium,
        medium_rates[None],
    )
    return jnp.transpose(copied(out), (1, 0, 2))[None]


def solution(mesh):
    in_specs = (
        P("phase", "ctx", None, "mp"),
        P(),
        P(None, None, "mp"),
        P(None, "mp"),
        P(None, None, "mp"),
        P(None, "mp"),
        P("mp"),
    )
    out_specs = P("phase", "ctx", None, "mp")
    return jax.shard_map(local, mesh=mesh, in_specs=in_specs, out_specs=out_specs, check_vma=False)
```

```python
import functools
import math

import jax
import jax.numpy as jnp
from jax import lax
from jax.experimental import pallas as pl
from jax.experimental.pallas import tpu as pltpu
from jax.sharding import PartitionSpec as P

HEAD_DIM = 128
CHUNKS = 4
HALO = 16
PIECES = 4
LANES = 128
MESH = pl.DeviceIdType.MESH


def feature(rows, weight, stream, count):
    first = rows.shape[0] - count
    return (
        weight[stream, 0][None] * rows[first:]
        + weight[stream, 1][None] * rows[first - 1 : first - 1 + count]
        + weight[stream, 2][None] * rows[first - 2 : first - 2 + count]
    )


def tick_kernel(
    hops,
    whole_ref,
    doc_ref,
    feat_all,
    filt_all,
    feat2_all,
    filt2_all,
    rate_all,
    out_ref,
    feat_ref,
    filt_ref,
    feat2_ref,
    filt2_ref,
    rate_ref,
    state,
    chain,
    halo,
    halo2,
    past,
    short,
    tail,
    shift_ref,
    h_ref,
    bias_ref,
    local_sems,
    send_sems,
    recv_sems,
):
    rows = state.shape[2]
    half = state.shape[3]
    width = half // CHUNKS
    tiles = width // LANES
    taps = filt2_ref.shape[0]
    keys = rows * (hops + 1)
    phase = lax.axis_index("phase")
    place = lax.axis_index("ctx")
    peers = lax.axis_size("ctx")
    right, left = place + 1, place - 1
    partner = 1 - phase
    has_left, has_right = place > 0, place < peers - 1

    mine = partner * half
    theirs = phase * half

    def piece(offset, size):
        return pl.ds(pl.multiple_of(offset, LANES), size)

    loads = [
        pltpu.make_async_copy(
            whole_ref.at[:, :, piece(mine, half)], state.at[phase], local_sems.at[CHUNKS]
        )
    ]
    pairs = (
        (feat_all.at[:, :, piece(mine, half)], feat_ref),
        (filt_all.at[:, piece(mine, half)], filt_ref),
        (feat2_all.at[:, :, piece(mine, half)], feat2_ref),
        (filt2_all.at[:, piece(mine, half)], filt2_ref),
        (rate_all.at[:, piece(mine, half)], rate_ref),
    )
    for index, (source, target) in enumerate(pairs):
        loads.append(pltpu.make_async_copy(source, target, local_sems.at[CHUNKS + 1 + index]))

    barrier = pltpu.get_barrier_semaphore()
    pl.semaphore_signal(barrier, inc=1, device_id={"phase": partner}, device_id_type=MESH)

    @pl.when(has_left)
    def _():
        pl.semaphore_signal(barrier, inc=1, device_id={"ctx": left}, device_id_type=MESH)

    @pl.when(has_right)
    def _():
        pl.semaphore_signal(barrier, inc=1, device_id={"ctx": right}, device_id_type=MESH)

    inner = (place + peers - 1) // peers + (peers - 1 - place + peers - 1) // peers
    pl.semaphore_wait(barrier, 1 + inner)

    def columns(chunk):
        return pl.ds(chunk * width, width)

    def remote(source, target, slot, device):
        return pltpu.make_async_remote_copy(
            src_ref=source,
            dst_ref=target,
            send_sem=send_sems.at[slot],
            recv_sem=recv_sems.at[slot],
            device_id=device,
            device_id_type=MESH,
        )

    per = hops + 6
    to_right = {"ctx": right}
    to_partner = {"phase": partner}

    def swap(c):
        return remote(
            whole_ref.at[:, :, piece(theirs + c * width, width)], state.at[phase, :, :, columns(c)], c * per, to_partner
        )

    def hop(c, s):
        source = (
            state.at[1, pl.ds(1, 2), :, columns(c)]
            if s == 0
            else chain.at[s - 1, :, :, columns(c)]
        )
        return remote(source, chain.at[s, :, :, columns(c)], c * per + 6 + s, to_right)

    def send_halo(c):
        rows_ref = state.at[0, :, pl.ds(rows - HALO, HALO), columns(c)]
        return remote(rows_ref, halo.at[:, :, columns(c)], c * per + 1, to_right)

    def send_halo2(c):
        rows_ref = short.at[:, pl.ds(rows - HALO, HALO), columns(c)]
        return remote(rows_ref, halo2.at[:, :, columns(c)], c * per + 2, to_right)

    def send_past(c):
        return remote(tail.at[:, columns(c)], past.at[:, columns(c)], c * per + 3, to_right)

    def send_pair(c):
        return remote(
            state.at[phase, pl.ds(0, 2), :, columns(c)],
            out_ref.at[pl.ds(0, 2), :, piece(mine + c * width, width)],
            c * per + 4,
            to_partner,
        )

    def send_value(c):
        return remote(
            state.at[phase, pl.ds(2, 1), :, columns(c)],
            out_ref.at[pl.ds(2, 1), :, piece(mine + c * width, width)],
            c * per + 5,
            to_partner,
        )

    def keep(c):
        return pltpu.make_async_copy(
            state.at[partner, :, :, columns(c)],
            out_ref.at[:, :, piece(mine + c * width, width)],
            local_sems.at[c],
        )

    for c in range(CHUNKS):
        swap(c).start()
    for load in loads:
        load.start()

    @pl.when(place == 0)
    def _():
        halo[...] = jnp.zeros_like(halo)
        halo2[...] = jnp.zeros_like(halo2)
        past[...] = jnp.zeros_like(past)

    for s in range(hops):

        @pl.when(place <= s)
        def _():
            chain[s] = jnp.zeros(chain.shape[1:], chain.dtype)

    def start(condition, *copies):
        @pl.when(condition)
        def _():
            for copy in copies:
                copy.start()

    def sent(condition, *copies):
        @pl.when(condition)
        def _():
            for copy in copies:
                copy.wait_send()

    def arrived(condition, *copies):
        @pl.when(condition)
        def _():
            for copy in copies:
                copy.wait_recv()

    def sends_hop(s):
        return has_right & (place >= s)

    column = lax.broadcasted_iota(jnp.int32, (rows, rows), 1)
    row = lax.broadcasted_iota(jnp.int32, (rows, rows), 0)
    docs = doc_ref[...].astype(jnp.float32)

    def block_docs(block):
        found = jnp.full((1, rows), -1.0, jnp.float32)
        for b in range(peers):
            found = jnp.where(block == b, docs[:, b * rows : (b + 1) * rows], found)
        return found

    own_docs = block_docs(place)
    query_doc = jnp.sum(jnp.where(column == row, own_docs, 0.0), axis=1, keepdims=True)
    for i in range(hops + 1):
        allowed = block_docs(place - hops + i) == query_doc
        if i == hops:
            allowed = allowed & (column <= row)
        bias_ref[:, i * rows : (i + 1) * rows] = jnp.where(allowed, 0.0, -1e30)

    def over_tiles(chunk, body):
        def one(index, carry):
            body(pl.ds(pl.multiple_of(chunk * width + index * LANES, LANES), LANES))
            return carry

        lax.fori_loop(0, tiles, one, 0)

    def earlier(block):
        return block.astype(jnp.float32)

    def short_tile(col):
        weight = feat_ref[:, :, col]

        def wide(stream):
            return jnp.concatenate(
                [earlier(halo[stream, :, col]), state[0, stream, :, col].astype(jnp.float32)], 0
            )

        count = rows + 8
        query = feature(wide(0), weight, 0, rows)
        key = feature(wide(1), weight, 1, count)
        value = feature(wide(2), weight, 2, count)
        product = (key * value).astype(jnp.bfloat16).astype(jnp.float32)
        filt = filt_ref[:, col]
        mixed = filt[0][None] * product[8:]
        for j in range(1, filt_ref.shape[0]):
            mixed += filt[j][None] * product[8 - j : 8 - j + rows]
        new_key = key[8:].astype(jnp.bfloat16)
        new_value = (state[0, 2, :, col].astype(jnp.float32) + query * mixed).astype(jnp.bfloat16)
        short[0, :, col] = query.astype(jnp.bfloat16)
        short[1, :, col] = new_key
        short[2, :, col] = new_value
        weight2 = feat2_ref[:, :, col]
        tail_key = feature(new_key.astype(jnp.float32), weight2, 1, taps)
        tail_value = feature(new_value.astype(jnp.float32), weight2, 2, taps)
        tail[:, col] = (tail_key * tail_value).astype(jnp.bfloat16)

    def medium_tile(col):
        weight = feat2_ref[:, :, col]

        def wide(stream):
            return jnp.concatenate(
                [earlier(halo2[stream, :, col]), short[stream, :, col].astype(jnp.float32)], 0
            )

        query = feature(wide(0), weight, 0, rows)
        key = feature(wide(1), weight, 1, rows)
        value = feature(wide(2), weight, 2, rows)
        state[0, 0, :, col] = query.astype(jnp.bfloat16)
        state[0, 1, :, col] = key.astype(jnp.bfloat16)
        shift_ref[0, :taps] = earlier(past[:, col])
        shift_ref[0, taps:] = (key * value).astype(jnp.bfloat16).astype(jnp.float32)
        length = taps + rows
        for r in range(1, 8):
            shift_ref[r, 8:] = shift_ref[0, 8 - r : length - r]
        position = lax.broadcasted_iota(jnp.int32, (taps, LANES), 0).astype(jnp.float32)
        h_ref[...] = filt2_ref[:, col] * jnp.exp(-rate_ref[:, col] * position)

        def step(m, total):
            weights = h_ref[pl.ds(pl.multiple_of(8 * m, 8), 8), :]
            first = pl.multiple_of(taps - 8 * m, 8)
            for r in range(8):
                total += weights[r : r + 1] * shift_ref[r, pl.ds(first, rows), :]
            return total

        mixed = lax.fori_loop(0, taps // 8, step, jnp.zeros((rows, LANES), jnp.float32))
        total = short[2, :, col].astype(jnp.float32) + query * mixed
        state[0, 2, :, col] = total.astype(jnp.bfloat16)

    def attention_tile(col):
        scale = 1.0 / math.sqrt(HEAD_DIM)
        order = list(range(hops))[::-1]
        key = jnp.concatenate([chain[s, 0, :, col] for s in order] + [state[1, 1, :, col]], 0)
        value = jnp.concatenate([chain[s, 1, :, col] for s in order] + [state[1, 2, :, col]], 0)
        scores = lax.dot_general(
            state[1, 0, :, col], key, (((1,), (1,)), ((), ())), preferred_element_type=jnp.float32
        )
        scores = scores * scale + bias_ref[...]
        exponent = jnp.exp(scores - jnp.max(scores, axis=1, keepdims=True))
        total = jnp.sum(exponent, axis=1, keepdims=True)
        attended = jnp.dot(exponent.astype(jnp.bfloat16), value, preferred_element_type=jnp.float32)
        attended = (attended / total).astype(jnp.bfloat16).astype(jnp.float32)
        summed = state[1, 2, :, col].astype(jnp.float32) + attended
        state[1, 2, :, col] = summed.astype(jnp.bfloat16)

    for load in loads:
        load.wait()
    last = 2 * (CHUNKS - 1) + hops
    for slot in range(last + 2):
        for c in range(CHUNKS):
            age = slot - 2 * c
            if age == 0:
                swap(c).wait_recv()
                start(has_right, hop(c, 0), send_halo(c))
            if 1 <= age <= hops:
                arrived(place >= age, hop(c, age - 1))
                if age < hops:
                    start(sends_hop(age), hop(c, age))
            if age == 3:
                send_pair(c).start()
            if age == hops + 1:
                send_value(c).start()
                keep(c).start()
        for c in range(CHUNKS):
            age = slot - 2 * c
            if age == 1:
                arrived(has_left, send_halo(c))
                over_tiles(c, short_tile)
                start(has_right, send_halo2(c), send_past(c))
        for c in range(CHUNKS):
            age = slot - 2 * c
            if age == hops:
                sent(has_right, hop(c, 0))
                over_tiles(c, attention_tile)
        for c in range(CHUNKS):
            age = slot - 2 * c
            if age == 2:
                arrived(has_left, send_halo2(c), send_past(c))
                sent(has_right, send_halo(c))
                over_tiles(c, medium_tile)

    for c in range(CHUNKS):
        swap(c).wait_send()
        sent(has_right, send_halo2(c), send_past(c))
        for s in range(1, hops):
            sent(sends_hop(s), hop(c, s))
        keep(c).wait()
        send_pair(c).wait()
        send_value(c).wait()


def copy_kernel(source, target, held, in_sems, out_sems):
    streams, rows, _ = source.shape
    size = rows // PIECES
    parts = [(i, pl.ds(j * size, size)) for i in range(streams) for j in range(PIECES)]
    ins = [
        pltpu.make_async_copy(source.at[part], held.at[part], in_sems.at[n])
        for n, part in enumerate(parts)
    ]
    outs = [
        pltpu.make_async_copy(held.at[part], target.at[part], out_sems.at[n])
        for n, part in enumerate(parts)
    ]
    for copy in ins:
        copy.start()
    for first, second in zip(ins, outs):
        first.wait()
        second.start()
    for copy in outs:
        copy.wait()


def copied(array):
    anywhere = pl.BlockSpec(memory_space=pl.ANY)
    count = array.shape[0] * PIECES
    return pl.pallas_call(
        copy_kernel,
        in_specs=[anywhere],
        out_specs=anywhere,
        out_shape=jax.ShapeDtypeStruct(array.shape, array.dtype),
        scratch_shapes=[
            pltpu.VMEM(array.shape, array.dtype),
            pltpu.SemaphoreType.DMA((count,)),
            pltpu.SemaphoreType.DMA((count,)),
        ],
    )(array)


def local(streams, doc_ids, feat_short, filt_short, feat_medium, filt_medium, medium_rates):
    rows = streams.shape[1]
    channels = streams.shape[3]
    half = channels // 2
    taps = filt_medium.shape[0]
    seq_total = rows * lax.axis_size("ctx")
    hops = -(-(seq_total // 2 - 1) // rows)
    keys = (hops + 1) * rows
    state = jnp.transpose(streams[0], (1, 0, 2))
    anywhere = pl.BlockSpec(memory_space=pl.ANY)
    inside = pl.BlockSpec(memory_space=pltpu.VMEM)
    slots = CHUNKS * (hops + 6)
    out = pl.pallas_call(
        functools.partial(tick_kernel, hops),
        in_specs=[anywhere, inside] + [anywhere] * 5,
        out_specs=anywhere,
        out_shape=jax.ShapeDtypeStruct((3, rows, channels), jnp.bfloat16),
        scratch_shapes=[
            pltpu.VMEM((3, 3, half), jnp.float32),
            pltpu.VMEM((filt_short.shape[0], half), jnp.float32),
            pltpu.VMEM((3, 3, half), jnp.float32),
            pltpu.VMEM((taps, half), jnp.float32),
            pltpu.VMEM((1, half), jnp.float32),
            pltpu.VMEM((2, 3, rows, half), jnp.bfloat16),
            pltpu.VMEM((hops, 2, rows, half), jnp.bfloat16),
            pltpu.VMEM((3, HALO, half), jnp.bfloat16),
            pltpu.VMEM((3, HALO, half), jnp.bfloat16),
            pltpu.VMEM((taps, half), jnp.bfloat16),
            pltpu.VMEM((3, rows, half), jnp.bfloat16),
            pltpu.VMEM((taps, half), jnp.bfloat16),
            pltpu.VMEM((8, taps + rows, LANES), jnp.float32),
            pltpu.VMEM((taps, LANES), jnp.float32),
            pltpu.VMEM((rows, keys), jnp.float32),
            pltpu.SemaphoreType.DMA((CHUNKS + 6,)),
            pltpu.SemaphoreType.DMA((slots,)),
            pltpu.SemaphoreType.DMA((slots,)),
        ],
        compiler_params=pltpu.CompilerParams(
            collective_id=0, has_side_effects=True, vmem_limit_bytes=62 * 1024 * 1024
        ),
    )(
        state,
        doc_ids[None],
        feat_short,
        filt_short,
        feat_medium,
        filt_medium,
        medium_rates[None],
    )
    return jnp.transpose(copied(out), (1, 0, 2))[None]


def solution(mesh):
    in_specs = (
        P("phase", "ctx", None, "mp"),
        P(),
        P(None, None, "mp"),
        P(None, "mp"),
        P(None, None, "mp"),
        P(None, "mp"),
        P("mp"),
    )
    out_specs = P("phase", "ctx", None, "mp")
    return jax.shard_map(local, mesh=mesh, in_specs=in_specs, out_specs=out_specs, check_vma=False)
```
